32 devices in a mesh: row: 8 (over z, y), col: 4 (over x, core).
Axes of the slice: x: 2, y: 2, z: 4, core: 2. Of those that a mesh axis runs over, the one named last changes fastest.
Arguments:
- basis_values: bfloat16 [128, 1024, 640], P(('row', 'col')), may hold values from -6 to 6
- potential: float32 [128, 1024], P(('row', 'col')), may hold values from -0.12 to 0.12
- block_lists: int32 [128, 5], P(('row', 'col')), may hold values from 0 to 63, as said below
- func_counts: int32 [128], P(('row', 'col')), may hold values from 576 to 640
- density_tiles: bfloat16 [8, 8, 16, 4, 128, 128], P(None, 'row', None, 'col'), may hold values from -0.0095825195 to 0.0095825195
Outputs:
- hamiltonian_tiles: float32 [8, 8, 16, 4, 128, 128], P(None, 'row', None, 'col')
- density_points: float32 [128, 1024], P(('row', 'col'))
The draws below stay inside these ranges and needn't reach their ends.
Inputs may be any that keep to these rules, and one draw needn't show every extreme that they name: `block_lists`: each batch lists 5 different blocks whose remainders modulo 8 are 5 consecutive values (counted cyclically) starting at an even number; the 4 batches of one device start at the remainders 0, 2, ..., 6, each exactly once, in an order drawn from the seed; the quotients of the blocks by 8 are free. So in the batches of one device no owner (block row modulo 8, block column modulo 4) of a listed pair of blocks is named by more than 5 pairs, and some owner is named by exactly 5.
All inputs are finite; a program needn't handle non-finite values.
Results may differ from the reference program's by a relative error of at most 0.0029.
Values may be sent and summed in bfloat16 or wider, within the bound.
A program may use at most 320 MiB of HBM per device.

```python
import jax
import jax.numpy as jnp
from jax import lax

BLOCK = 128
LIST_BLOCKS = 5
PTS = 1024
LIST = 640
NBLK = 64
BATCH_DEV = 4
BATCHES = 128
N_ROW = 8
N_COL = 4
DEVICES = 32


def draw_block_lists(key, part):
    first_key = jax.random.fold_in(key, 11)
    second_key = jax.random.fold_in(key, 23)
    scores = jax.random.randint(first_key, (DEVICES, BATCH_DEV), 0, 1 << 20)
    scores = scores * BATCH_DEV + jnp.arange(BATCH_DEV, dtype=jnp.int32)[None, :]
    order = jnp.argsort(scores, axis=1, stable=True).astype(jnp.int32)
    starts = 2 * order
    offsets = jnp.arange(LIST_BLOCKS, dtype=jnp.int32)
    residues = (starts[:, :, None] + offsets[None, None, :]) % N_ROW
    highs = jax.random.randint(second_key, (DEVICES, BATCH_DEV, LIST_BLOCKS), 0, NBLK // N_ROW)
    listed = residues + N_ROW * highs
    return listed.reshape(DEVICES * BATCH_DEV, LIST_BLOCKS).astype(jnp.int32)


def plant(values, rng, low, top_value):
    extent = values.shape
    spot = [jax.random.randint(jax.random.fold_in(rng, axis), (), 0, extent[axis]) for axis in range(len(extent))]
    values = values.at[tuple(spot)].set(low)
    longest = extent.index(max(extent))
    spot[longest] = (spot[longest] + 1) % extent[longest]
    return values.at[tuple(spot)].set(top_value)


def shard_levels(rng, extent, shards, smallest, top_value):
    def one(dim, parts):
        draws = jax.random.uniform(jax.random.fold_in(jax.random.fold_in(rng, 6), dim), (parts,), jnp.float32, smallest / len(shards), top_value / len(shards))
        return jnp.repeat(jnp.exp(draws), extent[dim] // parts).reshape((-1,) + (1,) * (len(extent) - dim - 1))

    level = one(*shards[0])
    for cut in shards[1:]:
        level = level * one(*cut)
    return level


def noise(rng, dims, scale, reach, shards=(), kind=jnp.bfloat16):
    loudness = shard_levels(rng, dims, shards, -0.22, 0.18) if shards else 1.0
    array = jax.random.normal(rng, dims, jnp.float32) * scale * loudness
    return jnp.minimum(jnp.maximum(array, -reach), reach).astype(kind)


def setup_inputs(seed: int = 0) -> dict:
    streams_of = jax.random.split(jax.random.key(seed), 6)
    basis_values = noise(streams_of[0], (BATCHES, PTS, LIST), 1.0, 6.0, ((0, 32),))
    potential = noise(streams_of[1], (BATCHES, PTS), 0.02, 0.12, ((0, 32),), jnp.float32)
    block_lists = draw_block_lists(jax.random.fold_in(streams_of[5], 71), 0)
    func_counts = plant(jax.random.randint(streams_of[3], (BATCHES,), LIST - BLOCK // 2, LIST + 1), jax.random.fold_in(streams_of[3], 1), LIST - BLOCK // 2, LIST).astype(jnp.int32)
    density_tiles = noise(streams_of[4], (NBLK // N_ROW, N_ROW, NBLK // N_COL, N_COL, BLOCK, BLOCK), 0.0016, 0.0095825195, ((1, 8), (3, 4)))
    return dict(basis_values=basis_values, potential=potential, block_lists=block_lists, func_counts=func_counts, density_tiles=density_tiles)


def reference(basis_values, potential, block_lists, func_counts, density_tiles):
    columns = jnp.arange(LIST, dtype=jnp.int32)
    empty = jnp.zeros((NBLK // N_ROW, N_ROW, NBLK // N_COL, N_COL, BLOCK, BLOCK), jnp.float32)

    def one_batch(totals, items):
        values, weight, listed, count = items
        keep = (columns < count)[None, :]
        masked = jnp.where(keep, values, jnp.zeros_like(values))
        weighted = (masked.astype(jnp.float32) * weight[:, None]).astype(jnp.bfloat16)
        local = jnp.dot(masked.T, weighted, preferred_element_type=jnp.float32)
        pieces = local.reshape(LIST_BLOCKS, BLOCK, LIST_BLOCKS, BLOCK).transpose(0, 2, 1, 3)
        first = listed[:, None] * jnp.ones((1, LIST_BLOCKS), jnp.int32)
        second = listed[None, :] * jnp.ones((LIST_BLOCKS, 1), jnp.int32)
        totals = totals.at[first // N_ROW, first % N_ROW, second // N_COL, second % N_COL].add(pieces)
        fetched = density_tiles[first // N_ROW, first % N_ROW, second // N_COL, second % N_COL]
        gathered = fetched.transpose(0, 2, 1, 3).reshape(LIST, LIST)
        product = jnp.dot(masked, gathered, preferred_element_type=jnp.float32)
        density = jnp.sum(product * masked.astype(jnp.float32), axis=1)
        return totals, density

    totals, density = lax.scan(one_batch, empty, (basis_values, potential, block_lists, func_counts))
    return totals, density
```

```python
import functools

import jax
import jax.numpy as jnp
from jax import lax
from jax.experimental import pallas as pl
from jax.experimental.pallas import tpu as pltpu
from jax.sharding import PartitionSpec as P

MESH = pl.DeviceIdType.MESH
VMEM_LIMIT = 60 * 1024 * 1024


def exchange_kernel(
    rows_n,
    cols_n,
    lists_ref,
    counts_ref,
    basis_ref,
    pot_ref,
    tiles_ref,
    arrived_ref,
    lists_out,
    dens_ref,
    xs,
    ws,
    hst,
    dst,
    gathered,
    myrow,
    landed,
    alllists,
    perm_s,
    list_send,
    list_recv,
    list_local,
    h_send,
    h_recv,
    d_send,
    d_recv,
):
    nbatch, points, width = basis_ref.shape
    block = tiles_ref.shape[-1]
    nl = width // block
    ndev = rows_n * cols_n
    reps = pl.cdiv(nl, cols_n)
    heads = (nl + 1) // 2
    my_r = lax.axis_index("row")
    my_c = lax.axis_index("col")
    me = my_r * cols_n + my_c

    def dev(d):
        return {"row": d // cols_n, "col": d % cols_n}

    barrier = pltpu.get_barrier_semaphore()

    @pl.loop(1, ndev)
    def _(i):
        d = (me + i) % ndev
        pl.semaphore_signal(barrier, inc=1, device_id=dev(d), device_id_type=MESH)

    listed = [[lists_ref[b, k] for k in range(nl)] for b in range(nbatch)]
    starts, sorted_val, sorted_pos = [], [], []
    for b in range(nbatch):
        res = [v % rows_n for v in listed[b]]
        start = jnp.int32(0)
        for k in range(nl):
            pred = (res[k] + (rows_n - 1)) % rows_n
            seen = functools.reduce(
                jnp.logical_or, [pred == res[j] for j in range(nl) if j != k]
            )
            start = start + jnp.where(seen, 0, res[k])
        starts.append(start)
        offs = [(r - start + rows_n) % rows_n for r in res]
        sorted_val.append(
            [sum(jnp.where(offs[k] == o, listed[b][k], 0) for k in range(nl)) for o in range(nl)]
        )
        sorted_pos.append(
            [sum(jnp.where(offs[k] == o, k, 0) for k in range(nl)) for o in range(nl)]
        )
    lane = lax.broadcasted_iota(jnp.int32, (1, block), 1)
    row = jnp.zeros((1, block), jnp.int32)
    for t in range(nbatch):
        hit = [starts[b] == 2 * t for b in range(nbatch)]
        order = jnp.minimum(sum(jnp.where(hit[b], b, 0) for b in range(nbatch)), nbatch - 1)
        perm_s[t, nl] = order
        row = jnp.where(lane == nbatch * nl + t, order, row)
        for o in range(nl):
            perm_s[t, o] = sum(jnp.where(hit[b], sorted_pos[b][o], 0) for b in range(nbatch))
            value = sum(jnp.where(hit[b], sorted_val[b][o], 0) for b in range(nbatch))
            row = jnp.where(lane == t * nl + o, value, row)
    myrow[...] = row

    def h_compute(t):
        b = perm_s[t, nl]
        count = counts_ref[b]
        pot = pot_ref[b]
        pot_col = jnp.transpose(jnp.broadcast_to(pot, (block, points)))
        for o in range(nl):
            k = perm_s[t, o]
            xf = jnp.zeros((points, block), jnp.float32)
            for p in range(nl):
                live = jnp.logical_and(lane + p * block < count, k == p)
                xb = basis_ref[b, :, p * block : (p + 1) * block]
                xf = xf + xb.astype(jnp.float32) * jnp.where(live, 1.0, 0.0)
            xs[t, :, o * block : (o + 1) * block] = xf.astype(jnp.bfloat16)
            ws[:, o * block : (o + 1) * block] = (xf * pot_col).astype(jnp.bfloat16)
        local = lax.dot_general(
            xs[t], ws[...], (((0,), (0,)), ((), ())), preferred_element_type=jnp.float32
        )
        for k in range(nl):
            for l in range(nl):
                hst[t, k, l] = local[
                    k * block : (k + 1) * block, l * block : (l + 1) * block
                ].astype(jnp.bfloat16)

    def h_copy(t, i):
        k, l = i // nl, i % nl
        r = (2 * t + k) % rows_n
        c = (2 * t + l) % cols_n
        slot = (k // 2) * reps + l // cols_n
        return (
            r * cols_n + c,
            lambda: pltpu.make_async_remote_copy(
                src_ref=hst.at[t, k, l],
                dst_ref=arrived_ref.at[slot, me],
                send_sem=h_send,
                recv_sem=h_recv.at[slot],
                device_id={"row": r, "col": c},
                device_id_type=MESH,
            ),
            lambda: pltpu.make_async_copy(
                hst.at[t, k, l], arrived_ref.at[slot, me], h_recv.at[slot]
            ),
        )

    def h_start(t):
        @pl.loop(0, nl * nl)
        def _(i):
            d, remote, local = h_copy(t, i)

            @pl.when(d != me)
            def _():
                remote().start()

            @pl.when(d == me)
            def _():
                local().start()

    def list_copy(d):
        return pltpu.make_async_remote_copy(
            src_ref=myrow,
            dst_ref=landed.at[me],
            send_sem=list_send,
            recv_sem=list_recv,
            device_id=dev(d),
            device_id_type=MESH,
        )

    pl.semaphore_wait(barrier, ndev - 1)

    @pl.loop(1, ndev)
    def _(i):
        list_copy((me + i) % ndev).start()

    own = pltpu.make_async_copy(myrow, landed.at[me], list_recv)
    own.start()

    turn = my_r // 2 + my_c

    def t_of(i):
        return (turn + i) % nbatch

    h_compute(t_of(0))
    h_start(t_of(0))

    pltpu.make_async_copy(landed, landed, list_recv).wait()
    to_smem = pltpu.make_async_copy(landed, alllists, list_local)
    to_smem.start()
    to_smem.wait()

    def slots(action):
        for j in range(heads):
            k = 2 * j + my_r % 2
            t = (my_r // 2 - j + nbatch) % nbatch
            for q in range(reps):
                l = (my_c - 2 * t + 2 * nbatch * cols_n) % cols_n + q * cols_n

                @pl.when(jnp.logical_and(k < nl, l < nl))
                def _(j=j, q=q, k=k, l=l, t=t):
                    action(j * reps + q, t, k, l)

    @pl.loop(0, ndev)
    def _(i):
        d = (me + i) % ndev

        def stage(slot, t, k, l):
            first = alllists[d, 0, t * nl + k]
            second = alllists[d, 0, t * nl + l]
            dst[slot, d] = tiles_ref[first // rows_n, second // cols_n]

        slots(stage)

    def place(t, k, l):
        return gathered.at[
            t,
            pl.ds(pl.multiple_of(k * block, block), block),
            pl.ds(pl.multiple_of(l * block, block), block),
        ]

    def d_remote(slot, t, k, l, d):
        return pltpu.make_async_remote_copy(
            src_ref=dst.at[slot, d],
            dst_ref=place(t, k, l),
            send_sem=d_send.at[slot],
            recv_sem=d_recv.at[t],
            device_id=dev(d),
            device_id_type=MESH,
        )

    def d_local(slot, t, k, l):
        return pltpu.make_async_copy(dst.at[slot, me], place(t, k, l), d_recv.at[t])

    @pl.loop(1, ndev)
    def _(i):
        d = (me + i) % ndev
        slots(lambda slot, t, k, l: d_remote(slot, t, k, l, d).start())

    slots(lambda slot, t, k, l: d_local(slot, t, k, l).start())

    @pl.loop(1, nbatch)
    def _(i):
        h_compute(t_of(i))
        h_start(t_of(i))

    lists_out[...] = landed[...]

    chunk = min(256, points)

    @pl.loop(0, nbatch)
    def _(i):
        t = t_of(i)
        pltpu.make_async_copy(gathered.at[t], gathered.at[t], d_recv.at[t]).wait()
        for s in range(points // chunk):
            x = xs[t, s * chunk : (s + 1) * chunk, :]
            prod = jnp.dot(x, gathered[t], preferred_element_type=jnp.float32)
            prod = prod * x.astype(jnp.float32)
            part = prod[:, :block]
            for o in range(1, nl):
                part = part + prod[:, o * block : (o + 1) * block]
            dens_ref[t, :, s * chunk : (s + 1) * chunk] = jnp.sum(
                jnp.transpose(part), axis=0, keepdims=True
            )

    slots(
        lambda slot, t, k, l: pltpu.make_async_copy(
            arrived_ref.at[slot], arrived_ref.at[slot], h_recv.at[slot]
        ).wait()
    )
    slots(
        lambda slot, t, k, l: pltpu.make_async_copy(
            dst.at[slot, pl.ds(0, ndev - 1)], dst.at[slot, pl.ds(0, ndev - 1)], d_send.at[slot]
        ).wait()
    )

    @pl.loop(0, nbatch * nl * nl)
    def _(i):
        d, remote, _ = h_copy(i // (nl * nl), i % (nl * nl))

        @pl.when(d != me)
        def _():
            remote().wait_send()

    pltpu.make_async_copy(
        landed.at[pl.ds(0, ndev - 1)], landed.at[pl.ds(0, ndev - 1)], list_send
    ).wait()


def scatter_kernel(rows_n, cols_n, nbatch, nl, lists_ref, arrived_ref, dens_in, ham_ref, dens_ref):
    ndev = rows_n * cols_n
    reps = pl.cdiv(nl, cols_n)
    heads = (nl + 1) // 2
    tile_cols = ham_ref.shape[1]
    my_r = lax.axis_index("row")
    my_c = lax.axis_index("col")
    me = my_r * cols_n + my_c

    @pl.loop(0, ham_ref.shape[0])
    def _(i):
        @pl.loop(0, tile_cols)
        def _(j):
            ham_ref[i, j] = jnp.zeros(ham_ref.shape[2:], jnp.float32)

    @pl.loop(0, ndev)
    def _(d):
        for j in range(heads):
            k = 2 * j + my_r % 2
            t = (my_r // 2 - j + nbatch) % nbatch
            for q in range(reps):
                l = (my_c - 2 * t + 2 * nbatch * cols_n) % cols_n + q * cols_n

                @pl.when(jnp.logical_and(k < nl, l < nl))
                def _(j=j, q=q, k=k, l=l, t=t):
                    i0 = lists_ref[d, 0, t * nl + k] // rows_n
                    j0 = lists_ref[d, 0, t * nl + l] // cols_n
                    ham_ref[i0, j0] += arrived_ref[j * reps + q, d].astype(jnp.float32)

    for t in range(nbatch):
        b = lists_ref[me, 0, nbatch * nl + t]
        dens_ref[pl.ds(b, 1), :] = dens_in[t]


def on_device(basis_values, potential, block_lists, func_counts, density_tiles):
    rows_n = lax.axis_size("row")
    cols_n = lax.axis_size("col")
    ndev = rows_n * cols_n
    nbatch, points, width = basis_values.shape
    nl = block_lists.shape[1]
    tile_rows, _, tile_cols, _, block, _ = density_tiles.shape
    assert nbatch * 2 == rows_n and rows_n % cols_n == 0
    nslots = (nl + 1) // 2 * pl.cdiv(nl, cols_n)
    tiles = density_tiles.reshape(tile_rows, tile_cols, block, block)
    vmem = pl.BlockSpec(memory_space=pltpu.VMEM)
    smem = pl.BlockSpec(memory_space=pltpu.SMEM)
    hbm = pl.BlockSpec(memory_space=pl.ANY)
    bf16 = jnp.bfloat16
    dma = pltpu.SemaphoreType.DMA
    arrived, lists, dens = pl.pallas_call(
        functools.partial(exchange_kernel, rows_n, cols_n),
        out_shape=(
            jax.ShapeDtypeStruct((nslots, ndev, block, block), bf16),
            jax.ShapeDtypeStruct((ndev, 1, block), jnp.int32),
            jax.ShapeDtypeStruct((nbatch, 1, points), jnp.float32),
        ),
        in_specs=[smem, smem, vmem, vmem, vmem],
        out_specs=(hbm, vmem, vmem),
        scratch_shapes=[
            pltpu.VMEM((nbatch, points, width), bf16),
            pltpu.VMEM((points, width), bf16),
            pltpu.VMEM((nbatch, nl, nl, block, block), bf16),
            pltpu.VMEM((nslots, ndev, block, block), bf16),
            pltpu.VMEM((nbatch, width, width), bf16),
            pltpu.VMEM((1, block), jnp.int32),
            pltpu.VMEM((ndev, 1, block), jnp.int32),
            pltpu.SMEM((ndev, 1, block), jnp.int32),
            pltpu.SMEM((nbatch, nl + 1), jnp.int32),
            dma,
            dma,
            dma,
            dma,
            dma((nslots,)),
            dma((nslots,)),
            dma((nbatch,)),
        ],
        compiler_params=pltpu.CompilerParams(
            collective_id=0, has_side_effects=True, vmem_limit_bytes=VMEM_LIMIT
        ),
    )(block_lists, func_counts, basis_values, potential.reshape(nbatch, 1, points), tiles)
    ham, density_points = pl.pallas_call(
        functools.partial(scatter_kernel, rows_n, cols_n, nbatch, nl),
        out_shape=(
            jax.ShapeDtypeStruct((tile_rows, tile_cols, block, block), jnp.float32),
            jax.ShapeDtypeStruct((nbatch, points), jnp.float32),
        ),
        in_specs=[smem, vmem, vmem],
        out_specs=(vmem, vmem),
        compiler_params=pltpu.CompilerParams(vmem_limit_bytes=VMEM_LIMIT),
    )(lists, arrived, dens)
    return ham.reshape(tile_rows, 1, tile_cols, 1, block, block), density_points


def solution(mesh):
    in_specs = (
        P(("row", "col"), None, None),
        P(("row", "col"), None),
        P(("row", "col"), None),
        P(("row", "col")),
        P(None, "row", None, "col", None, None),
    )
    out_specs = (P(None, "row", None, "col", None, None), P(("row", "col"), None))
    return jax.shard_map(
        on_device, mesh=mesh, in_specs=in_specs, out_specs=out_specs, check_vma=False
    )
```

```python
import functools
import math

import jax
import jax.numpy as jnp
from jax import lax
from jax.experimental import pallas as pl
from jax.experimental.pallas import tpu as pltpu
from jax.sharding import PartitionSpec as P

MESH = pl.DeviceIdType.MESH
VMEM_LIMIT = 60 * 1024 * 1024


def exchange_kernel(
    rows_n,
    cols_n,
    lists_ref,
    counts_ref,
    basis_ref,
    pot_ref,
    tiles_ref,
    arrived_ref,
    lists_out,
    dens_ref,
    xs,
    ws,
    hst,
    dst,
    gathered,
    myrow,
    landed,
    alllists,
    perm_s,
    list_send,
    list_recv,
    list_local,
    h_send,
    h_recv,
    d_send,
    d_recv,
):
    nbatch, points, width = basis_ref.shape
    block = tiles_ref.shape[-1]
    nl = width // block
    ndev = rows_n * cols_n
    reps = pl.cdiv(nl, cols_n)
    heads = (nl + 1) // 2
    my_r = lax.axis_index("row")
    my_c = lax.axis_index("col")
    me = my_r * cols_n + my_c

    def dev(d):
        return {"row": d // cols_n, "col": d % cols_n}

    barrier = pltpu.get_barrier_semaphore()

    @pl.loop(1, ndev)
    def _(i):
        d = (me + i) % ndev
        pl.semaphore_signal(barrier, inc=1, device_id=dev(d), device_id_type=MESH)

    listed = [[lists_ref[b, k] for k in range(nl)] for b in range(nbatch)]
    starts, sorted_val, sorted_pos = [], [], []
    for b in range(nbatch):
        res = [v % rows_n for v in listed[b]]
        start = jnp.int32(0)
        for k in range(nl):
            pred = (res[k] + (rows_n - 1)) % rows_n
            seen = functools.reduce(
                jnp.logical_or, [pred == res[j] for j in range(nl) if j != k]
            )
            start = start + jnp.where(seen, 0, res[k])
        starts.append(start)
        offs = [(r - start + rows_n) % rows_n for r in res]
        sorted_val.append(
            [sum(jnp.where(offs[k] == o, listed[b][k], 0) for k in range(nl)) for o in range(nl)]
        )
        sorted_pos.append(
            [sum(jnp.where(offs[k] == o, k, 0) for k in range(nl)) for o in range(nl)]
        )
    lane = lax.broadcasted_iota(jnp.int32, (1, block), 1)
    row = jnp.zeros((1, block), jnp.int32)
    for t in range(nbatch):
        hit = [starts[b] == 2 * t for b in range(nbatch)]
        order = jnp.minimum(sum(jnp.where(hit[b], b, 0) for b in range(nbatch)), nbatch - 1)
        perm_s[t, nl] = order
        row = jnp.where(lane == nbatch * nl + t, order, row)
        for o in range(nl):
            perm_s[t, o] = sum(jnp.where(hit[b], sorted_pos[b][o], 0) for b in range(nbatch))
            value = sum(jnp.where(hit[b], sorted_val[b][o], 0) for b in range(nbatch))
            row = jnp.where(lane == t * nl + o, value, row)
    myrow[...] = row

    def h_compute(t):
        b = perm_s[t, nl]
        count = counts_ref[b]
        pot = pot_ref[b]
        pot_col = jnp.transpose(jnp.broadcast_to(pot, (block, points)))
        for o in range(nl):
            k = perm_s[t, o]
            xf = jnp.zeros((points, block), jnp.float32)
            for p in range(nl):
                live = jnp.logical_and(lane + p * block < count, k == p)
                xb = basis_ref[b, :, p * block : (p + 1) * block]
                xf = xf + xb.astype(jnp.float32) * jnp.where(live, 1.0, 0.0)
            xs[t, :, o * block : (o + 1) * block] = xf.astype(jnp.bfloat16)
            ws[:, o * block : (o + 1) * block] = (xf * pot_col).astype(jnp.bfloat16)
        local = lax.dot_general(
            xs[t], ws[...], (((0,), (0,)), ((), ())), preferred_element_type=jnp.float32
        )
        for k in range(nl):
            for l in range(nl):
                hst[t, k, l] = local[
                    k * block : (k + 1) * block, l * block : (l + 1) * block
                ].astype(jnp.bfloat16)

    def h_copy(t, i):
        k, l = i % nl, i // nl
        r = (2 * t + k) % rows_n
        c = (2 * t + l) % cols_n
        slot = (k // 2) * reps + l // cols_n
        return (
            r * cols_n + c,
            lambda: pltpu.make_async_remote_copy(
                src_ref=hst.at[t, k, l],
                dst_ref=arrived_ref.at[slot, me],
                send_sem=h_send,
                recv_sem=h_recv.at[slot],
                device_id={"row": r, "col": c},
                device_id_type=MESH,
            ),
            lambda: pltpu.make_async_copy(
                hst.at[t, k, l], arrived_ref.at[slot, me], h_recv.at[slot]
            ),
        )

    def h_start(t):
        @pl.loop(0, nl * nl)
        def _(i):
            d, remote, local = h_copy(t, i)

            @pl.when(d != me)
            def _():
                remote().start()

            @pl.when(d == me)
            def _():
                local().start()

    def list_copy(d):
        return pltpu.make_async_remote_copy(
            src_ref=myrow,
            dst_ref=landed.at[me],
            send_sem=list_send,
            recv_sem=list_recv,
            device_id=dev(d),
            device_id_type=MESH,
        )

    pl.semaphore_wait(barrier, ndev - 1)

    @pl.loop(1, ndev)
    def _(i):
        list_copy((me + i) % ndev).start()

    own = pltpu.make_async_copy(myrow, landed.at[me], list_recv)
    own.start()

    turn = my_r // 2 + nbatch // 2

    def t_of(i):
        return (turn + i) % nbatch

    h_compute(t_of(0))
    h_start(t_of(0))

    pltpu.make_async_copy(landed, landed, list_recv).wait()
    to_smem = pltpu.make_async_copy(landed, alllists, list_local)
    to_smem.start()
    to_smem.wait()

    def slots(action):
        for j in range(heads):
            k = 2 * j + my_r % 2
            t = (my_r // 2 - j + nbatch) % nbatch
            for q in range(reps):
                l = (my_c - 2 * t + 2 * nbatch * cols_n) % cols_n + q * cols_n

                @pl.when(jnp.logical_and(k < nl, l < nl))
                def _(j=j, q=q, k=k, l=l, t=t):
                    action(j * reps + q, t, k, l)

    @pl.loop(0, ndev)
    def _(i):
        d = (me + i) % ndev

        def stage(slot, t, k, l):
            first = alllists[d, 0, t * nl + k]
            second = alllists[d, 0, t * nl + l]
            dst[slot, d] = tiles_ref[first // rows_n, second // cols_n]

        slots(stage)

    def place(t, k, l):
        return gathered.at[
            t,
            pl.ds(pl.multiple_of(k * block, block), block),
            pl.ds(pl.multiple_of(l * block, block), block),
        ]

    def d_remote(slot, t, k, l, d):
        return pltpu.make_async_remote_copy(
            src_ref=dst.at[slot, d],
            dst_ref=place(t, k, l),
            send_sem=d_send.at[slot],
            recv_sem=d_recv.at[t],
            device_id=dev(d),
            device_id_type=MESH,
        )

    def d_local(slot, t, k, l):
        return pltpu.make_async_copy(dst.at[slot, me], place(t, k, l), d_recv.at[t])

    stride = next(s for s in range(2 * ndev // 5, 2 * ndev) if math.gcd(s, ndev) == 1)

    @pl.loop(1, ndev)
    def _(i):
        d = (me + i * stride) % ndev
        slots(lambda slot, t, k, l: d_remote(slot, t, k, l, d).start())

    slots(lambda slot, t, k, l: d_local(slot, t, k, l).start())

    @pl.loop(1, nbatch)
    def _(i):
        h_compute(t_of(i))
        h_start(t_of(i))

    lists_out[...] = landed[...]

    chunk = min(256, points)

    @pl.loop(0, nbatch)
    def _(i):
        t = t_of(i)
        pltpu.make_async_copy(gathered.at[t], gathered.at[t], d_recv.at[t]).wait()
        for s in range(points // chunk):
            x = xs[t, s * chunk : (s + 1) * chunk, :]
            prod = jnp.dot(x, gathered[t], preferred_element_type=jnp.float32)
            prod = prod * x.astype(jnp.float32)
            part = prod[:, :block]
            for o in range(1, nl):
                part = part + prod[:, o * block : (o + 1) * block]
            dens_ref[t, :, s * chunk : (s + 1) * chunk] = jnp.sum(
                jnp.transpose(part), axis=0, keepdims=True
            )

    slots(
        lambda slot, t, k, l: pltpu.make_async_copy(
            arrived_ref.at[slot], arrived_ref.at[slot], h_recv.at[slot]
        ).wait()
    )
    slots(
        lambda slot, t, k, l: pltpu.make_async_copy(
            dst.at[slot, pl.ds(0, ndev - 1)], dst.at[slot, pl.ds(0, ndev - 1)], d_send.at[slot]
        ).wait()
    )

    @pl.loop(0, nbatch * nl * nl)
    def _(i):
        d, remote, _ = h_copy(i // (nl * nl), i % (nl * nl))

        @pl.when(d != me)
        def _():
            remote().wait_send()

    pltpu.make_async_copy(
        landed.at[pl.ds(0, ndev - 1)], landed.at[pl.ds(0, ndev - 1)], list_send
    ).wait()


def scatter_kernel(
    rows_n, cols_n, nbatch, nl, lists_ref, arrived_ref, dens_in, ham_ref, dens_ref, held, sems
):
    ndev = rows_n * cols_n
    reps = pl.cdiv(nl, cols_n)
    heads = (nl + 1) // 2
    tile_cols = ham_ref.shape[1]
    my_r = lax.axis_index("row")
    my_c = lax.axis_index("col")
    me = my_r * cols_n + my_c

    def slots(action):
        for j in range(heads):
            k = 2 * j + my_r % 2
            t = (my_r // 2 - j + nbatch) % nbatch
            for q in range(reps):
                l = (my_c - 2 * t + 2 * nbatch * cols_n) % cols_n + q * cols_n

                @pl.when(jnp.logical_and(k < nl, l < nl))
                def _(j=j, q=q, k=k, l=l, t=t):
                    action(j * reps + q, t, k, l)

    def load(slot):
        return pltpu.make_async_copy(arrived_ref.at[slot], held.at[slot], sems.at[slot])

    slots(lambda slot, t, k, l: load(slot).start())

    @pl.loop(0, ham_ref.shape[0])
    def _(i):
        @pl.loop(0, tile_cols)
        def _(j):
            ham_ref[i, j] = jnp.zeros(ham_ref.shape[2:], jnp.float32)

    def add(slot, t, k, l):
        load(slot).wait()

        @pl.loop(0, ndev)
        def _(d):
            i0 = lists_ref[d, 0, t * nl + k] // rows_n
            j0 = lists_ref[d, 0, t * nl + l] // cols_n
            ham_ref[i0, j0] += held[slot, d].astype(jnp.float32)

    slots(add)

    for t in range(nbatch):
        b = lists_ref[me, 0, nbatch * nl + t]
        dens_ref[pl.ds(b, 1), :] = dens_in[t]


def on_device(basis_values, potential, block_lists, func_counts, density_tiles):
    rows_n = lax.axis_size("row")
    cols_n = lax.axis_size("col")
    ndev = rows_n * cols_n
    nbatch, points, width = basis_values.shape
    nl = block_lists.shape[1]
    tile_rows, _, tile_cols, _, block, _ = density_tiles.shape
    assert nbatch * 2 == rows_n and rows_n % cols_n == 0
    nslots = (nl + 1) // 2 * pl.cdiv(nl, cols_n)
    tiles = density_tiles.reshape(tile_rows, tile_cols, block, block)
    vmem = pl.BlockSpec(memory_space=pltpu.VMEM)
    smem = pl.BlockSpec(memory_space=pltpu.SMEM)
    hbm = pl.BlockSpec(memory_space=pl.ANY)
    bf16 = jnp.bfloat16
    dma = pltpu.SemaphoreType.DMA
    arrived, lists, dens = pl.pallas_call(
        functools.partial(exchange_kernel, rows_n, cols_n),
        out_shape=(
            jax.ShapeDtypeStruct((nslots, ndev, block, block), bf16),
            jax.ShapeDtypeStruct((ndev, 1, block), jnp.int32),
            jax.ShapeDtypeStruct((nbatch, 1, points), jnp.float32),
        ),
        in_specs=[smem, smem, vmem, vmem, vmem],
        out_specs=(hbm, vmem, vmem),
        scratch_shapes=[
            pltpu.VMEM((nbatch, points, width), bf16),
            pltpu.VMEM((points, width), bf16),
            pltpu.VMEM((nbatch, nl, nl, block, block), bf16),
            pltpu.VMEM((nslots, ndev, block, block), bf16),
            pltpu.VMEM((nbatch, width, width), bf16),
            pltpu.VMEM((1, block), jnp.int32),
            pltpu.VMEM((ndev, 1, block), jnp.int32),
            pltpu.SMEM((ndev, 1, block), jnp.int32),
            pltpu.SMEM((nbatch, nl + 1), jnp.int32),
            dma,
            dma,
            dma,
            dma,
            dma((nslots,)),
            dma((nslots,)),
            dma((nbatch,)),
        ],
        compiler_params=pltpu.CompilerParams(
            collective_id=0, has_side_effects=True, vmem_limit_bytes=VMEM_LIMIT
        ),
    )(block_lists, func_counts, basis_values, potential.reshape(nbatch, 1, points), tiles)
    ham, density_points = pl.pallas_call(
        functools.partial(scatter_kernel, rows_n, cols_n, nbatch, nl),
        out_shape=(
            jax.ShapeDtypeStruct((tile_rows, tile_cols, block, block), jnp.float32),
            jax.ShapeDtypeStruct((nbatch, points), jnp.float32),
        ),
        in_specs=[smem, hbm, vmem],
        out_specs=(vmem, vmem),
        scratch_shapes=[pltpu.VMEM((nslots, ndev, block, block), bf16), dma((nslots,))],
        compiler_params=pltpu.CompilerParams(vmem_limit_bytes=VMEM_LIMIT),
    )(lists, arrived, dens)
    return ham.reshape(tile_rows, 1, tile_cols, 1, block, block), density_points


def solution(mesh):
    in_specs = (
        P(("row", "col"), None, None),
        P(("row", "col"), None),
        P(("row", "col"), None),
        P(("row", "col")),
        P(None, "row", None, "col", None, None),
    )
    out_specs = (P(None, "row", None, "col", None, None), P(("row", "col"), None))
    return jax.shard_map(
        on_device, mesh=mesh, in_specs=in_specs, out_specs=out_specs, check_vma=False
    )
```
